32 devices in a mesh: dp: 8 (over z, x), seq: 4 (over y, core).
Axes of the slice: x: 2, y: 2, z: 4, core: 2. Of those that a mesh axis runs over, the one named last changes fastest.
Arguments:
- tokens: bfloat16 [2, 8, 1024, 1536], P(None, 'dp', 'seq'), may hold values from -6 to 6
- query_weight: bfloat16 [1536, 768], P('dp'), may hold values from -0.01953125 to 0.01953125
- key_weight: bfloat16 [1536, 768], P('dp'), may hold values from -0.15625 to 0.15625
- value_weight: bfloat16 [1536, 768], P('dp'), may hold values from -0.15625 to 0.15625
- mix_weight: bfloat16 [768, 1536], P('dp'), may hold values from -6 to 6
- gate_weight: bfloat16 [1536, 3968], P('dp'), may hold values from -0.15625 to 0.15625
- up_weight: bfloat16 [1536, 3968], P('dp'), may hold values from -0.15625 to 0.15625
- down_weight: bfloat16 [3968, 1536], P('dp'), may hold values from -0.09375 to 0.09375
- attn_gain: bfloat16 [1536], P('dp'), may hold values from 0.5 to 1.5
- ffn_gain: bfloat16 [1536], P('dp'), may hold values from 0.5 to 1.5
- bias_table: float32 [32, 12], P(None, 'seq'), may hold values from -4 to 4
- bucket_ids: int32 [2048], replicated, may hold values from 0 to 31, as said below
- out_grad: bfloat16 [2, 8, 1024, 1536], P(None, 'dp', 'seq'), may hold values from -6 to 6
Outputs:
- output: bfloat16 [2, 8, 1024, 1536], P(None, 'dp', 'seq')
- input_grad: float32 [2, 8, 1024, 1536], P(None, 'dp', 'seq')
- grad_query: float32 [1536, 768], P('dp')
- grad_key: float32 [1536, 768], P('dp')
- grad_value: float32 [1536, 768], P('dp')
- grad_mix: float32 [768, 1536], P('dp')
- grad_gate: float32 [1536, 3968], P('dp')
- grad_up: float32 [1536, 3968], P('dp')
- grad_down: float32 [3968, 1536], P('dp')
- grad_attn_gain: float32 [1536], P('dp')
- grad_ffn_gain: float32 [1536], P('dp')
- grad_bias_table: float32 [32, 12], P(None, 'seq')
The draws below stay inside these ranges and needn't reach their ends.
Inputs may be any that keep to these rules, and one draw needn't show every extreme that they name: bucket_ids[j] is the bucket of the key-minus-query offset j - 1024: offsets 0 to 7 apart have a bucket each, farther offsets share 8 more buckets by distance, the last of them beginning at most 128 apart; positive offsets add half of 32.
All inputs are finite; a program needn't handle non-finite values.
Results may differ from the reference program's by a relative error of at most 0.017.
Values may be sent and summed in bfloat16 or wider, within the bound.
No kernel may reach another device: no remote copies, remote signals or barrier semaphores. Data moves between devices by JAX's collectives and lax.ppermute only.
A program may use at most 320 MiB of HBM per device.

```python
import math
from functools import partial
import jax
import jax.numpy as jnp
from jax import lax

D = 1536
H = 12
DK = 64
FF = 3968
NB = 32
LEN = 1024
MICRO = 2
NSEQ = 8
INNER = 768
MAXD = 128


def draw_bucket_ids(key, part):
    spread_factor = jax.random.permutation(key, jnp.arange(9, MAXD + 1, dtype=jnp.int32))[:7]
    cut_points = jnp.concatenate([jnp.arange(1, 9, dtype=jnp.int32), spread_factor])
    offsets = jnp.arange(2 * LEN, dtype=jnp.int32) - LEN
    distance = jnp.abs(offsets)
    far_count = jnp.sum((distance[:, None] >= cut_points[None, :]).astype(jnp.int32), axis=1)
    return far_count + NB // 2 * (offsets > 0).astype(jnp.int32)


def strengthened(drawn, key, source, target, shards_of, factor):
    def block_of(dim):
        return (jnp.arange(drawn.shape[dim]) // (drawn.shape[dim] // shards_of)).reshape((-1,) + (1,) * (drawn.ndim - 1 - dim))

    first = jax.random.permutation(key, shards_of)[block_of(target)]
    far = (block_of(target) + shards_of // 2) % shards_of
    return jnp.where((block_of(source) == first) | (block_of(source) == far), factor * drawn, drawn)


def block_scale(key, dims, shards, low, largest):
    loudness = 1.0
    for dim, shards_of in shards:
        steps = jax.random.uniform(jax.random.fold_in(jax.random.fold_in(key, 6), dim), (shards_of,), jnp.float32, low / len(shards), largest / len(shards))
        loudness = loudness * jnp.repeat(jnp.exp(steps), dims[dim] // shards_of).reshape((-1,) + (1,) * (len(dims) - 1 - dim))
    return loudness


def centred(key, extent, spread, limit, cuts=(), kind=jnp.bfloat16):
    values = spread * jax.random.normal(key, extent, jnp.float32)
    if cuts:
        values = values * block_scale(key, extent, cuts, -0.22, 0.18)
    return jnp.clip(values, -limit, limit).astype(kind)


def gaussian_with(key, dims, scale, reach, cuts, heavy, held_as=jnp.bfloat16):
    entries = scale * jax.random.normal(key, dims, jnp.float32)
    if cuts:
        entries = entries * block_scale(key, dims, cuts, -0.22, 0.18)
    return jnp.clip(strengthened(entries, jax.random.fold_in(key, 3), *heavy), -reach, reach).astype(held_as)


def setup_inputs(seed: int = 0) -> dict:
    key_of = jax.random.split(jax.random.key(seed), 14)
    tokens = gaussian_with(key_of[0], (MICRO, NSEQ, LEN, D), 1.0, 6.0, ((1, 8), (2, 4)), (1, 3, 8, 2.0))
    query_weight = centred(key_of[1], (D, INNER), (D * DK) ** -0.5, 0.01953125, ((0, 8),))
    key_weight = centred(key_of[2], (D, INNER), D ** -0.5, 0.15625, ((0, 8),))
    value_weight = centred(key_of[3], (D, INNER), D ** -0.5, 0.15625, ((0, 8),))
    mix_weight = centred(key_of[4], (INNER, D), 1.0, 6.0, ((0, 8),))
    gate_weight = centred(key_of[5], (D, FF), D ** -0.5, 0.15625, ((0, 8),))
    up_weight = centred(key_of[6], (D, FF), D ** -0.5, 0.15625, ((0, 8),))
    down_weight = centred(key_of[7], (FF, D), FF ** -0.5, 0.09375, ((0, 8),))
    attn_gain = jnp.clip(1.0 + 0.1 * jax.random.normal(key_of[8], (D,), jnp.float32), 0.5, 1.5).astype(jnp.bfloat16)
    ffn_gain = jnp.clip(1.0 + 0.1 * jax.random.normal(key_of[9], (D,), jnp.float32), 0.5, 1.5).astype(jnp.bfloat16)
    bias_table = centred(key_of[10], (NB, H), 1.0, 4.0, ((1, 4),), jnp.float32)
    bucket_ids = draw_bucket_ids(jax.random.fold_in(key_of[13], 71), 0)
    out_grad = centred(key_of[12], (MICRO, NSEQ, LEN, D), 1.0, 6.0, ((1, 8), (2, 4)))
    return {"tokens": tokens, "query_weight": query_weight, "key_weight": key_weight, "value_weight": value_weight, "mix_weight": mix_weight, "gate_weight": gate_weight, "up_weight": up_weight, "down_weight": down_weight, "attn_gain": attn_gain, "ffn_gain": ffn_gain, "bias_table": bias_table, "bucket_ids": bucket_ids, "out_grad": out_grad}


epsilon = 1e-06
gelu_scale = 0.7978845608028654
gelu_cubic = 0.044715

@jax.custom_vjp
def low(v):
    return lax.optimization_barrier(v.astype(jnp.bfloat16)).astype(jnp.float32)

@jax.custom_vjp
def low_back(v):
    return v

def low_keep(v):
    return (low(v), None)

def low_pass(kept, grad):
    return (grad,)

def back_keep(v):
    return (v, None)

def back_low(kept, grad):
    return (low(grad),)
low.defvjp(low_keep, low_pass)
low_back.defvjp(back_keep, back_low)

def both_ways(tensor):
    return low(low_back(tensor))

def matmul(left_operand, right_operand):
    return jnp.einsum('gld,de->gle', left_operand, right_operand, precision=lax.Precision.HIGHEST)

def rms_scale(features, gain):
    return features * lax.rsqrt(lax.optimization_barrier(jnp.mean(features * features, axis=-1, keepdims=True)) + epsilon) * gain

def gelu_tanh(gate_pre):
    return 0.5 * gate_pre * (1.0 + jnp.tanh(gelu_scale * (gate_pre + gelu_cubic * gate_pre * gate_pre * gate_pre)))

def attend_one(head_bias, triple):
    query_rows, key_rows, value_rows = triple
    length = query_rows.shape[0]
    query_heads = query_rows.reshape(length, H, DK)
    key_heads = key_rows.reshape(length, H, DK)
    value_heads = value_rows.reshape(length, H, DK)
    scores = jnp.einsum('qhd,khd->hqk', query_heads, key_heads, precision=lax.Precision.HIGHEST) + head_bias
    scores = low_back(scores)
    attn_probs = low(jax.nn.softmax(scores, axis=-1))
    attended = jnp.einsum('hqk,khd->qhd', attn_probs, value_heads, precision=lax.Precision.HIGHEST)
    return both_ways(attended.reshape(length, H * DK))

def encoder_layer(inputs, weight_bundle, bias_table, offset_ids):
    query_weight, key_weight, value_weight, mix_weight, gate_weight, up_weight, down_weight, attn_gain, ffn_gain = weight_bundle
    normed_attn = low(rms_scale(inputs, attn_gain))
    query_all = both_ways(matmul(normed_attn, query_weight))
    key_all = both_ways(matmul(normed_attn, key_weight))
    value_all = both_ways(matmul(normed_attn, value_weight))
    head_bias = jnp.transpose(bias_table[offset_ids], (2, 0, 1))
    attended = lax.map(jax.checkpoint(partial(attend_one, head_bias)), (query_all, key_all, value_all))
    middle = inputs + low_back(matmul(attended, mix_weight))
    normalized_feedforward = low(rms_scale(middle, ffn_gain))
    gate_pre = low_back(matmul(normalized_feedforward, gate_weight))
    up_pre = low_back(matmul(normalized_feedforward, up_weight))
    hidden = low(gelu_tanh(gate_pre) * up_pre)
    return middle + matmul(hidden, down_weight)

def reference(tokens, query_weight, key_weight, value_weight, mix_weight, gate_weight, up_weight, down_weight, attn_gain, ffn_gain, bias_table, bucket_ids, out_grad):
    seq_total = MICRO * NSEQ
    group_size = math.gcd(4, seq_total)
    shape_in = (seq_total // group_size, group_size, LEN, D)
    inputs = tokens.astype(jnp.float32).reshape(shape_in)
    cotangent = out_grad.astype(jnp.float32).reshape(shape_in)
    weight_bundle = tuple((weight_item.astype(jnp.float32) for weight_item in (query_weight, key_weight, value_weight, mix_weight, gate_weight, up_weight, down_weight, attn_gain, ffn_gain)))
    positions = jnp.arange(LEN, dtype=jnp.int32)
    offset_ids = bucket_ids[(positions[None, :] - positions[:, None] + LEN).astype(jnp.int32)]

    def whole_layer(layer_in, layer_weights, table):

        def one_group(group_rows):
            return encoder_layer(group_rows, layer_weights, table, offset_ids)
        return lax.map(jax.checkpoint(one_group), layer_in)
    result, pull_back = jax.vjp(whole_layer, inputs, weight_bundle, bias_table.astype(jnp.float32))
    input_grad, weight_grads, table_grad = pull_back(cotangent)
    grad_query, grad_key, grad_value, grad_mix, grad_gate, grad_up, grad_down, grad_attn_gain, grad_ffn_gain = weight_grads
    full_shape = (MICRO, NSEQ, LEN, D)
    output = result.reshape(full_shape).astype(jnp.bfloat16)
    input_grad = input_grad.reshape(full_shape)
    return (output, input_grad, grad_query, grad_key, grad_value, grad_mix, grad_gate, grad_up, grad_down, grad_attn_gain, grad_ffn_gain, table_grad)
```

```python
import functools

import jax
import jax.numpy as jnp
from jax import lax
from jax.experimental import pallas as pl
from jax.experimental.pallas import tpu as pltpu
from jax.sharding import PartitionSpec as P

epsilon = 1e-06
gelu_scale = 0.7978845608028654
gelu_cubic = 0.044715
low = jnp.bfloat16
wide = jnp.float32
lanes = 128


def rms_forward(features):
    inverse = lax.rsqrt(jnp.mean(features * features, axis=-1, keepdims=True) + epsilon)
    return (features * inverse, inverse)


def rms_backward(upstream, normed, inverse, gain):
    scaled = upstream * gain
    return inverse * (scaled - normed * jnp.mean(scaled * normed, axis=-1, keepdims=True))


def gelu_pair(gate_pre):
    inner_argument = gelu_scale * (gate_pre + gelu_cubic * gate_pre * gate_pre * gate_pre)
    tanh_part = jnp.tanh(inner_argument)
    gelu_value = 0.5 * gate_pre * (1.0 + tanh_part)
    gelu_slope = 0.5 * (1.0 + tanh_part) + 0.5 * gate_pre * (
        1.0 - tanh_part * tanh_part
    ) * gelu_scale * (1.0 + 3.0 * gelu_cubic * gate_pre * gate_pre)
    return (gelu_value, gelu_slope)


def mm(left, right, dims, out=low):
    return lax.dot_general(left, right, ((dims[:1], dims[1:]), ((), ())), preferred_element_type=wide).astype(out)


def flip_core(array):
    return lax.ppermute(array, "seq", [(0, 1), (1, 0), (2, 3), (3, 2)])


def flip_y(array):
    return lax.ppermute(array, "seq", [(0, 2), (2, 0), (1, 3), (3, 1)])


def flip_x(array):
    return lax.ppermute(array, "dp", [(d, d ^ 1) for d in range(8)])


def z_up(array, sources):
    return lax.ppermute(array, "dp", [(2 * z + x, 2 * z + 2 + x) for z in sources for x in (0, 1)])


def z_down(array, sources):
    return lax.ppermute(array, "dp", [(2 * z + x, 2 * z - 2 + x) for z in sources for x in (0, 1)])


def gather_dp(shard):
    if lax.axis_size("dp") != 8:
        return lax.all_gather(shard, "dp", axis=0, tiled=False)
    d = lax.axis_index("dp")
    z, x = d // 2, d % 2
    up1, down1, side0 = z_up(shard, (0, 1, 2)), z_down(shard, (1, 2, 3)), flip_x(shard)
    up2, down2 = z_up(up1, (1, 2)), z_down(down1, (2, 1))
    first = jnp.where(z == 0, down1, up1)
    side1 = flip_x(first)
    up3, down3 = z_up(up2, (2,)), z_down(down2, (1,))
    second = jnp.where(z == 0, down2, jnp.where(z == 3, up2, down1))
    side2 = flip_x(second)
    third = jnp.where(z == 0, down3, jnp.where(z == 1, down2, jnp.where(z == 2, up2, up3)))
    side3 = flip_x(third)
    at1 = jnp.where(z == 0, 1, z - 1)
    at2 = jnp.where(z == 0, 2, jnp.where(z == 3, 1, z + 1))
    at3 = jnp.where((z == 0) | (z == 1), 3, 0)
    whole = jnp.zeros((8,) + shard.shape, shard.dtype)
    for block, at, across in (
        (shard, z, x),
        (side0, z, 1 - x),
        (first, at1, x),
        (side1, at1, 1 - x),
        (second, at2, x),
        (side2, at2, 1 - x),
        (third, at3, x),
        (side3, at3, 1 - x),
    ):
        whole = lax.dynamic_update_slice(whole, block[None], (2 * at + across, 0, 0))
    return whole


def scatter_dp(parts):
    if lax.axis_size("dp") != 8:
        return lax.psum_scatter(parts, "dp", scatter_dimension=0, tiled=False)
    d = lax.axis_index("dp")
    z, x = d // 2, d % 2
    by_x = parts.reshape((4, 2) + parts.shape[1:])
    mine = lax.dynamic_index_in_dim(by_x, x, 1, keepdims=False)
    other = lax.dynamic_index_in_dim(by_x, 1 - x, 1, keepdims=False)
    mine = (mine.astype(wide) + flip_x(other).astype(wide)).astype(low)

    def block(index):
        return lax.dynamic_index_in_dim(mine, jnp.clip(index, 0, 3), 0, keepdims=False)

    def joined(left, right):
        return (left.astype(wide) + right.astype(wide)).astype(low)

    up, down = z_up(block(z + 3), (0,)), z_down(block(z - 3), (3,))
    up, down = z_up(joined(block(z + 2), up), (0, 1)), z_down(joined(block(z - 2), down), (3, 2))
    up, down = z_up(joined(block(z + 1), up), (0, 1, 2)), z_down(joined(block(z - 1), down), (3, 2, 1))
    return block(z).astype(wide) + up.astype(wide) + down.astype(wide)


def sum_dp(small):
    size = lax.axis_size("dp")
    step = 1
    while step < size:
        small = small + lax.ppermute(small, "dp", [(d, d ^ step) for d in range(size)])
        step *= 2
    return small


def gather_seq(block):
    pair = jnp.stack([block, flip_y(block)])
    return jnp.concatenate([pair, flip_core(pair)])


def scatter_seq(parts):
    back = flip_core(parts[2:4])
    away = (parts[1].astype(wide) + back[1].astype(wide)).astype(low)
    return parts[0].astype(wide) + back[0].astype(wide) + flip_y(away).astype(wide)


def by_slot(groups, s):
    grid = groups.reshape((2, 2) + groups.shape[1:])
    grid = jnp.swapaxes(grid, 0, 1)
    grid = jnp.where(s % 2 == 1, grid[::-1], grid)
    grid = jnp.where(s // 2 == 1, grid[:, ::-1], grid)
    return grid.reshape(groups.shape)


def by_index(slots, s):
    grid = slots.reshape((2, 2) + slots.shape[1:])
    grid = jnp.where(s % 2 == 1, grid[::-1], grid)
    grid = jnp.where(s // 2 == 1, grid[:, ::-1], grid)
    return jnp.swapaxes(grid, 0, 1).reshape(slots.shape)


def quarter_of(per):
    return -(-(-(-per // 4)) // 16) * 16


def pick_kernel(s_ref, gate_ref, up_ref, out_ref, *, owners, per, quarter):
    for choice in range(4):

        @pl.when(s_ref[0] == choice)
        def _():
            width = min(quarter, per - choice * quarter)
            for half, ref in enumerate((gate_ref, up_ref)):
                for d in range(owners):
                    start = d * per + choice * quarter
                    piece = ref[:, start : start + width]
                    if width < quarter:
                        piece = jnp.concatenate(
                            [piece, jnp.zeros((piece.shape[0], quarter - width), piece.dtype)], axis=1
                        )
                    to = (half * owners + d) * quarter
                    out_ref[:, to : to + quarter] = piece


def pick_columns(gate, up, s):
    owners = lax.axis_size("dp")
    rows, total = gate.shape
    per = total // owners
    quarter = quarter_of(per)
    if quarter % lanes:
        def one(weight):
            padded = jnp.pad(weight.reshape(rows, owners, per), ((0, 0), (0, 0), (0, 4 * quarter - per)))
            return lax.dynamic_slice_in_dim(padded, s * quarter, quarter, 2).reshape(rows, owners * quarter)

        return jnp.concatenate([one(gate), one(up)], axis=1)
    return pl.pallas_call(
        functools.partial(pick_kernel, owners=owners, per=per, quarter=quarter),
        out_shape=jax.ShapeDtypeStruct((rows, 2 * owners * quarter), gate.dtype),
        grid_spec=pltpu.PrefetchScalarGridSpec(
            num_scalar_prefetch=1,
            grid=(1,),
            in_specs=[pl.BlockSpec(gate.shape, lambda i, s: (0, 0))] * 2,
            out_specs=pl.BlockSpec((rows, 2 * owners * quarter), lambda i, s: (0, 0)),
        ),
        name="pick_columns",
    )(s.reshape(1), gate, up)


def place_kernel(parts_ref, gate_ref, up_ref, *, owners, per, quarter):
    for half, ref in enumerate((gate_ref, up_ref)):
        for d in range(owners):
            pieces = []
            for choice in range(4):
                width = min(quarter, per - choice * quarter)
                at = (half * owners + d) * quarter
                pieces.append(parts_ref[choice, :, at : at + width].astype(wide))
            ref[:, d * per : (d + 1) * per] = jnp.concatenate(pieces, axis=1)


def place_columns(parts, total):
    owners = lax.axis_size("dp")
    rows = parts.shape[1]
    per = total // owners
    quarter = quarter_of(per)
    if quarter % lanes:
        grid = parts.reshape(4, rows, 2, owners, quarter).transpose(2, 1, 3, 0, 4)
        flat = grid.reshape(2, rows, owners, 4 * quarter)[:, :, :, :per].reshape(2, rows, total)
        return (flat[0].astype(wide), flat[1].astype(wide))
    block = 96 if rows % 96 == 0 else rows
    return pl.pallas_call(
        functools.partial(place_kernel, owners=owners, per=per, quarter=quarter),
        out_shape=[jax.ShapeDtypeStruct((rows, total), wide)] * 2,
        grid=(rows // block,),
        in_specs=[pl.BlockSpec((4, block, parts.shape[2]), lambda i: (0, i, 0))],
        out_specs=[pl.BlockSpec((block, total), lambda i: (i, 0))] * 2,
        name="place_columns",
    )(parts)


def slot_index(slot, s):
    return s ^ (2 * (slot % 2) + slot // 2)


def toeplitz_kernel(offsets_ref, out_ref, *, block, heads):
    for head in range(heads):
        row = jnp.broadcast_to(offsets_ref[head : head + 1, :], (block, offsets_ref.shape[1]))
        width = row.shape[1]
        rolled = pltpu.roll(row, width - block, 1, stride=1, stride_axis=0)
        out_ref[head] = rolled[:, : width - block]


def toeplitz(per_offset, block):
    heads, width = per_offset.shape
    return pl.pallas_call(
        functools.partial(toeplitz_kernel, block=block, heads=heads),
        out_shape=jax.ShapeDtypeStruct((heads, block, width - block), wide),
        name="toeplitz",
    )(per_offset)


def forward_kernel(s_ref, rows_ref, all_ref, bias_ref, out_ref, probs_ref, *, heads, size, block):
    s = s_ref[0]
    here = slot_index(pl.program_id(0), s)
    inner = heads * size
    outs = []
    for head in range(heads):
        query = rows_ref[:, head * size : (head + 1) * size]
        key = all_ref[:, inner + head * size : inner + (head + 1) * size]
        value = all_ref[:, 2 * inner + head * size : 2 * inner + (head + 1) * size]
        scores = lax.dot_general(query, key, (((1,), (1,)), ((), ())), preferred_element_type=wide)
        pieces = []
        for slot in range(4):
            start = pl.multiple_of((slot_index(slot, s) - here + 3) * block, block)
            pieces.append(scores[:, slot * block : (slot + 1) * block] + bias_ref[head, :, pl.ds(start, block)])
        scores = jnp.concatenate(pieces, axis=1)
        expo = jnp.exp(scores - jnp.max(scores, axis=-1, keepdims=True))
        probs = (expo * (1.0 / jnp.sum(expo, axis=-1, keepdims=True))).astype(low)
        probs_ref[head] = probs
        outs.append(jnp.dot(probs, value, preferred_element_type=wide))
    out_ref[...] = jnp.concatenate(outs, axis=1).astype(low)


def attend_forward(mixed, bias, s, heads):
    length, columns = mixed.shape
    inner = columns // 3
    block = length // 4
    return pl.pallas_call(
        functools.partial(forward_kernel, heads=heads, size=inner // heads, block=block),
        out_shape=[
            jax.ShapeDtypeStruct((length, inner), low),
            jax.ShapeDtypeStruct((heads, length, length), low),
        ],
        grid_spec=pltpu.PrefetchScalarGridSpec(
            num_scalar_prefetch=1,
            grid=(4,),
            in_specs=[
                pl.BlockSpec((block, columns), lambda i, s: (i, 0)),
                pl.BlockSpec((length, columns), lambda i, s: (0, 0)),
                pl.BlockSpec(bias.shape, lambda i, s: (0, 0, 0)),
            ],
            out_specs=[
                pl.BlockSpec((block, inner), lambda i, s: (i, 0)),
                pl.BlockSpec((heads, block, length), lambda i, s: (0, i, 0)),
            ],
        ),
        cost_estimate=pl.CostEstimate(
            flops=16 * length * length * inner, transcendentals=heads * length * length,
            bytes_accessed=2 * heads * length * length + bias.size * 4,
        ),
        name="attend_forward",
    )(s.reshape(1), mixed, mixed, bias)


def backward_kernel(
    s_ref, rows_ref, all_ref, grad_ref, probs_ref, out_ref, sums_ref, key_ref, value_ref, *, heads, size, block
):
    s = s_ref[0]
    step = pl.program_id(0)
    here = slot_index(step, s)
    inner = heads * size

    @pl.when(step == 0)
    def _():
        sums_ref[...] = jnp.zeros_like(sums_ref)
        key_ref[...] = jnp.zeros_like(key_ref)
        value_ref[...] = jnp.zeros_like(value_ref)

    outs = []
    for head in range(heads):
        query = rows_ref[:, head * size : (head + 1) * size]
        key = all_ref[:, inner + head * size : inner + (head + 1) * size]
        value = all_ref[:, 2 * inner + head * size : 2 * inner + (head + 1) * size]
        grad = grad_ref[:, head * size : (head + 1) * size]
        probs_low = probs_ref[head]
        probs = probs_low.astype(wide)
        prob_grad = lax.dot_general(grad, value, (((1,), (1,)), ((), ())), preferred_element_type=wide)
        centred = jnp.sum(probs * prob_grad, axis=-1, keepdims=True)
        score_low = (probs * (prob_grad - centred)).astype(low)
        outs.append(jnp.dot(score_low, key, preferred_element_type=wide))
        key_ref[head] += lax.dot_general(query, score_low, (((0,), (0,)), ((), ())), preferred_element_type=wide)
        value_ref[head] += lax.dot_general(grad, probs_low, (((0,), (0,)), ((), ())), preferred_element_type=wide)
        for slot in range(4):
            start = pl.multiple_of((slot_index(slot, s) - here + 3) * block, block)
            sums_ref[head, :, pl.ds(start, block)] += score_low[:, slot * block : (slot + 1) * block].astype(wide)
    at = pl.multiple_of(step * block, block)
    out_ref[pl.ds(at, block), :inner] = jnp.concatenate(outs, axis=1).astype(low)

    @pl.when(step == 3)
    def _():
        turned = [key_ref[head].T for head in range(heads)] + [value_ref[head].T for head in range(heads)]
        out_ref[:, inner:] = jnp.concatenate(turned, axis=1).astype(low)


def attend_backward(mixed, grad, probs, s, heads):
    length, columns = mixed.shape
    inner = columns // 3
    block = length // 4
    size = inner // heads
    return pl.pallas_call(
        functools.partial(backward_kernel, heads=heads, size=size, block=block),
        out_shape=[
            jax.ShapeDtypeStruct((length, columns), low),
            jax.ShapeDtypeStruct((heads, block, 2 * length - block), wide),
        ],
        grid_spec=pltpu.PrefetchScalarGridSpec(
            num_scalar_prefetch=1,
            grid=(4,),
            in_specs=[
                pl.BlockSpec((block, columns), lambda i, s: (i, 0)),
                pl.BlockSpec((length, columns), lambda i, s: (0, 0)),
                pl.BlockSpec((block, inner), lambda i, s: (i, 0)),
                pl.BlockSpec((heads, block, length), lambda i, s: (0, i, 0)),
            ],
            out_specs=[
                pl.BlockSpec((length, columns), lambda i, s: (0, 0)),
                pl.BlockSpec((heads, block, 2 * length - block), lambda i, s: (0, 0, 0)),
            ],
            scratch_shapes=[pltpu.VMEM((heads, size, length), wide), pltpu.VMEM((heads, size, length), wide)],
        ),
        cost_estimate=pl.CostEstimate(
            flops=32 * length * length * inner, transcendentals=0,
            bytes_accessed=2 * heads * length * length + heads * block * length * 8,
        ),
        name="attend_backward",
    )(s.reshape(1), mixed, mixed, grad, probs)


def diagonal_kernel(*refs, heads, block):
    out_ref = refs[-1]
    width = refs[0].shape[2] + block
    for head in range(heads):
        total = refs[0][head]
        for ref in refs[1:-1]:
            total = total + ref[head]
        total = jnp.concatenate([total, jnp.zeros((block, block), wide)], axis=1)
        rows = block
        while rows > 8:
            rows //= 2
            total = total[:rows] + pltpu.roll(total[rows:], width - rows, 1)
        total = pltpu.roll(total, block, 1)
        line = total[0:1]
        for row in range(1, 8):
            line = line + pltpu.roll(total[row : row + 1], width - row, 1)
        out_ref[head : head + 1, :] = line


def diagonal_sums(sums):
    heads, block, width = sums[0].shape
    return pl.pallas_call(
        functools.partial(diagonal_kernel, heads=heads, block=block),
        out_shape=jax.ShapeDtypeStruct((heads, width + block), wide),
        name="diagonal_sums",
    )(*sums)


def ffn_kernel(x_ref, g_ref, gu_ref, down_ref, hidden_ref, grads_ref, *, width, tile):
    x = x_ref[...]
    g = g_ref[...]
    for start in range(0, width, tile):
        gate_pre = jnp.dot(x, gu_ref[:, start : start + tile], preferred_element_type=wide)
        up_pre = jnp.dot(x, gu_ref[:, width + start : width + start + tile], preferred_element_type=wide)
        hidden_grad = lax.dot_general(
            g, down_ref[start : start + tile, :], (((1,), (1,)), ((), ())), preferred_element_type=wide
        )
        gelu_value, gelu_slope = gelu_pair(gate_pre)
        hidden_ref[:, start : start + tile] = (gelu_value * up_pre).astype(low)
        grads_ref[:, start : start + tile] = (hidden_grad * up_pre * gelu_slope).astype(low)
        grads_ref[:, width + start : width + start + tile] = (hidden_grad * gelu_value).astype(low)


def feed_forward(x, g, gate_up, down):
    tokens, model = x.shape
    width = down.shape[0]
    rows = 256
    tile = 256
    return pl.pallas_call(
        functools.partial(ffn_kernel, width=width, tile=tile),
        out_shape=[
            jax.ShapeDtypeStruct((tokens, width), low),
            jax.ShapeDtypeStruct((tokens, 2 * width), low),
        ],
        grid=(tokens // rows,),
        in_specs=[
            pl.BlockSpec((rows, model), lambda i: (i, 0)),
            pl.BlockSpec((rows, model), lambda i: (i, 0)),
            pl.BlockSpec((model, 2 * width), lambda i: (0, 0)),
            pl.BlockSpec((width, model), lambda i: (0, 0)),
        ],
        out_specs=[
            pl.BlockSpec((rows, width), lambda i: (i, 0)),
            pl.BlockSpec((rows, 2 * width), lambda i: (i, 0)),
        ],
        cost_estimate=pl.CostEstimate(
            flops=6 * tokens * model * width, transcendentals=tokens * width,
            bytes_accessed=2 * (2 * tokens * model + 3 * model * width + 3 * tokens * width),
        ),
        name="feed_forward",
    )(x, g, gate_up, down)


def per_device(
    tokens,
    query_weight,
    key_weight,
    value_weight,
    mix_weight,
    gate_weight,
    up_weight,
    down_weight,
    attn_gain,
    ffn_gain,
    bias_table,
    bucket_ids,
    out_grad,
):
    owners = lax.axis_size("dp")
    s = lax.axis_index("seq")
    core = s % 2
    micro_count = tokens.shape[0]
    local, model = tokens.shape[2:]
    bucket_count, heads = bias_table.shape
    length = bucket_ids.shape[0] // 2
    hidden_total = gate_weight.shape[1]
    per = down_weight.shape[0]
    quarter = quarter_of(per)
    width = owners * quarter
    inner = query_weight.shape[1] // 4
    mix_rows = mix_weight.shape[0]

    shard_rows = query_weight.shape[0]
    own_heads = [lax.dynamic_slice_in_dim(w, s * inner, inner, 1) for w in (query_weight, key_weight, value_weight)]
    gains = jnp.pad(jnp.stack([attn_gain, ffn_gain], axis=1), ((0, 0), (0, 62)))
    qkv_gathered = gather_dp(jnp.concatenate(own_heads + [gains], axis=1)).reshape(model, 3 * inner + 64)
    full_qkv = qkv_gathered[:, : 3 * inner]
    gain_one = qkv_gathered[:, 3 * inner].astype(wide)
    gain_two = qkv_gathered[:, 3 * inner + 1].astype(wide)
    mix_half = gather_dp(lax.dynamic_slice_in_dim(mix_weight, core * (mix_rows // 2), mix_rows // 2, 0))
    mix_other = flip_core(mix_half)
    full_mix = jnp.stack(
        [jnp.where(core == 0, mix_half, mix_other), jnp.where(core == 0, mix_other, mix_half)], axis=1
    ).reshape(4, inner, model)
    slot_mix = by_slot(full_mix, s).reshape(4 * inner, model)
    full_gu = gather_dp(pick_columns(gate_weight, up_weight, s)).reshape(model, 2 * width)
    down_padded = jnp.pad(down_weight, ((0, 4 * quarter - per), (0, 0)))
    full_down = gather_dp(lax.dynamic_slice_in_dim(down_padded, s * quarter, quarter, 0)).reshape(width, model)

    onehot = (jnp.arange(bucket_count, dtype=jnp.int32)[:, None] == bucket_ids[None, :]).astype(wide)
    per_offset = lax.dot_general(
        bias_table, onehot, (((0,), (0,)), ((), ())), precision=lax.Precision.HIGHEST
    )
    bias = toeplitz(per_offset, local)

    saved = []
    for micro in range(micro_count):
        x = gather_seq(tokens[micro, 0]).reshape(length, model)
        features = x.astype(wide)
        normed, inverse = rms_forward(features)
        normed_low = (normed * gain_one).astype(low)
        mixed = mm(normed_low, full_qkv, (1, 0))
        attended, probs = attend_forward(mixed, bias, s, heads)
        blocks = attended.reshape(4, local, inner)
        from_y = flip_y(blocks)[jnp.array([1, 0, 3, 2])]
        from_core = flip_core(jnp.stack([blocks, from_y]))[:, jnp.array([2, 3, 0, 1])]
        attended_all = jnp.concatenate(
            [blocks, from_y, from_core[0], from_core[1]], axis=2
        ).reshape(length, 4 * inner)
        middle = features + mm(attended_all, slot_mix, (1, 0), wide)
        normed_middle, inverse_middle = rms_forward(middle)
        ffn_low = (normed_middle * gain_two).astype(low)
        saved.append((x, normed_low, mixed, probs, attended_all[:local], middle[:local], ffn_low))

    outputs, middle_grads, grads, hiddens, cotangents = [], [], [], [], []
    ffn_gain_sum = jnp.zeros((model,), wide)
    mix_ins, qkv_grads, diagonals, hidden_grads = [], [], [], []
    for micro in range(micro_count):
        x, normed_low, mixed, probs, attended_own, middle_own, ffn_low = saved[micro]
        g = gather_seq(out_grad[micro, 0]).reshape(length, model)
        hidden, hidden_grad = feed_forward(ffn_low, g, full_gu, full_down)
        ffn_in = scatter_seq(mm(hidden_grad, full_gu, (1, 1)).reshape(4, local, model))
        normed_middle, inverse_middle = rms_forward(middle_own)
        middle_grad = out_grad[micro, 0].astype(wide) + rms_backward(
            ffn_in, normed_middle, inverse_middle, gain_two
        )
        ffn_gain_sum = ffn_gain_sum + jnp.sum(ffn_in * normed_middle, axis=0)
        mix_in = middle_grad.astype(low)
        result = scatter_seq(mm(hidden, full_down, (1, 0)).reshape(4, local, model))
        outputs.append((middle_own + result).astype(low))
        attended_grad = mm(mix_in, slot_mix, (1, 1))
        far = flip_y(jnp.stack([attended_grad[:, inner : 2 * inner], attended_grad[:, 3 * inner :]]))
        near = flip_core(jnp.stack([attended_grad[:, 2 * inner : 3 * inner], far[1]]))
        own_grad = jnp.concatenate([attended_grad[:, :inner], far[0], near[0], near[1]], axis=0)
        qkv_grad, diagonal = attend_backward(mixed, own_grad, probs, s, heads)
        hiddens.append(hidden)
        hidden_grads.append(hidden_grad)
        cotangents.append(g)
        middle_grads.append(middle_grad)
        mix_ins.append(mix_in)
        qkv_grads.append(qkv_grad)
        diagonals.append(diagonal)

    all_ffn_low = jnp.concatenate([item[6] for item in saved])
    all_normed = jnp.concatenate([item[1] for item in saved])
    all_attended = jnp.concatenate([item[4] for item in saved])
    grad_gu = scatter_dp(mm(all_ffn_low, jnp.concatenate(hidden_grads), (0, 0)).reshape(owners, shard_rows, 2 * width))
    grad_down = scatter_dp(
        mm(jnp.concatenate(hiddens), jnp.concatenate(cotangents), (0, 0)).reshape(owners, quarter, model)
    )
    grad_mix = by_index(mm(all_attended, jnp.concatenate(mix_ins), (0, 0)).reshape(4, inner, model), s)
    grad_mix = grad_mix.reshape(owners, 2, mix_rows // 2, model)
    kept = lax.dynamic_index_in_dim(grad_mix, core, 1, keepdims=False)
    sent = lax.dynamic_index_in_dim(grad_mix, 1 - core, 1, keepdims=False)
    grad_mix = scatter_dp((kept.astype(wide) + flip_core(sent).astype(wide)).astype(low)).astype(low)

    input_grads = []
    attn_gain_sum = jnp.zeros((model,), wide)
    for micro in range(micro_count):
        x = saved[micro][0]
        partial = mm(qkv_grads[micro], full_qkv, (1, 1))
        normed, inverse = rms_forward(x.astype(wide))
        attn_gain_sum = attn_gain_sum + jnp.sum(partial.astype(wide) * normed, axis=0)
        attn_in = scatter_seq(partial.reshape(4, local, model))
        input_grads.append(
            middle_grads[micro] + rms_backward(attn_in, normed[:local], inverse[:local], gain_one)
        )
    gain_sums = jnp.pad(jnp.stack([attn_gain_sum, ffn_gain_sum], axis=1).astype(low), ((0, 0), (0, 62)))
    grad_qkv = scatter_dp(
        jnp.concatenate(
            [mm(all_normed, jnp.concatenate(qkv_grads), (0, 0)), gain_sums], axis=1
        ).reshape(owners, shard_rows, 3 * inner + 64)
    )

    grad_gate, grad_up = place_columns(by_index(gather_seq(grad_gu.astype(low)), s), hidden_total)
    grad_down = by_index(gather_seq(grad_down.astype(low)), s).reshape(4 * quarter, model)[:per].astype(wide)
    mix_sum = (grad_mix.astype(wide) + flip_y(grad_mix).astype(wide)).astype(low)
    mix_two = flip_core(mix_sum)
    grad_mix = jnp.concatenate(
        [jnp.where(core == 0, mix_sum, mix_two), jnp.where(core == 0, mix_two, mix_sum)]
    ).astype(wide)
    qkv_parts = by_index(gather_seq(grad_qkv.astype(low)), s).astype(wide)
    grad_query, grad_key, grad_value = (
        jnp.concatenate([qkv_parts[i, :, k * inner : (k + 1) * inner] for i in range(4)], axis=1) for k in range(3)
    )
    grad_gains = jnp.sum(qkv_parts[:, :, 3 * inner : 3 * inner + 2], axis=0)
    table_local = lax.dot_general(
        onehot, diagonal_sums(diagonals), (((1,), (1,)), ((), ())), precision=lax.Precision.HIGHEST
    )
    grad_bias_table = sum_dp(table_local)
    return (
        jnp.stack(outputs)[:, None],
        jnp.stack(input_grads)[:, None],
        grad_query,
        grad_key,
        grad_value,
        grad_mix,
        grad_gate,
        grad_up,
        grad_down,
        grad_gains[:, 0],
        grad_gains[:, 1],
        grad_bias_table,
    )


def solution(mesh):
    in_specs = (
        P(None, "dp", "seq", None),
        P("dp", None),
        P("dp", None),
        P("dp", None),
        P("dp", None),
        P("dp", None),
        P("dp", None),
        P("dp", None),
        P("dp"),
        P("dp"),
        P(None, "seq"),
        P(),
        P(None, "dp", "seq", None),
    )
    out_specs = (
        P(None, "dp", "seq", None),
        P(None, "dp", "seq", None),
        P("dp", None),
        P("dp", None),
        P("dp", None),
        P("dp", None),
        P("dp", None),
        P("dp", None),
        P("dp", None),
        P("dp"),
        P("dp"),
        P(None, "seq"),
    )
    return jax.shard_map(
        per_device, mesh=mesh, in_specs=in_specs, out_specs=out_specs, check_vma=False
    )
```

```python
import functools

import jax
import jax.numpy as jnp
from jax import lax
from jax.experimental import pallas as pl
from jax.experimental.pallas import tpu as pltpu
from jax.sharding import PartitionSpec as P

epsilon = 1e-06
gelu_scale = 0.7978845608028654
gelu_cubic = 0.044715
low = jnp.bfloat16
wide = jnp.float32
lanes = 128


def rms_forward(features):
    inverse = lax.rsqrt(jnp.mean(features * features, axis=-1, keepdims=True) + epsilon)
    return (features * inverse, inverse)


def rms_backward(upstream, normed, inverse, gain):
    scaled = upstream * gain
    return inverse * (scaled - normed * jnp.mean(scaled * normed, axis=-1, keepdims=True))


def gelu_pair(gate_pre):
    inner_argument = gelu_scale * (gate_pre + gelu_cubic * gate_pre * gate_pre * gate_pre)
    tanh_part = jnp.tanh(inner_argument)
    gelu_value = 0.5 * gate_pre * (1.0 + tanh_part)
    gelu_slope = 0.5 * (1.0 + tanh_part) + 0.5 * gate_pre * (
        1.0 - tanh_part * tanh_part
    ) * gelu_scale * (1.0 + 3.0 * gelu_cubic * gate_pre * gate_pre)
    return (gelu_value, gelu_slope)


def mm(left, right, dims, out=low):
    return lax.dot_general(left, right, ((dims[:1], dims[1:]), ((), ())), preferred_element_type=wide).astype(out)


def flip_core(array):
    return lax.ppermute(array, "seq", [(0, 1), (1, 0), (2, 3), (3, 2)])


def flip_y(array):
    return lax.ppermute(array, "seq", [(0, 2), (2, 0), (1, 3), (3, 1)])


class Later:
    value = None


class Rounds:
    def __init__(self):
        self.jobs, self.ended = [], ()

    def add(self, job, *operands, open_end=False):
        self.jobs.append((job, operands, open_end, Later()))
        return self.jobs[-1][3]

    def close(self):
        given = []
        for job, operands, open_end, later in self.jobs:
            given.append([o.value if isinstance(o, Later) else o for o in operands])
        given, unused = lax.optimization_barrier((given, self.ended))
        ended = []
        for (job, operands, open_end, later), arrays in zip(self.jobs, given):
            later.value = job(*arrays)
            if not open_end:
                ended.append(later.value)
        self.jobs, self.ended = [], ended


def flip_x(array):
    return lax.ppermute(array, "dp", [(d, d ^ 1) for d in range(8)])


def turn_z(array):
    return lax.ppermute(array, "dp", [(d, (d + 2) % 8) for d in range(8)])


def by_ring():
    return lax.axis_size("dp") == 8


def owner_order():
    d = lax.axis_index("dp")
    z, x = d // 2, d % 2
    return jnp.stack([2 * ((z - r) % 4) + (x if side == 0 else 1 - x) for r in range(4) for side in (0, 1)])


def ring_blocks(parts):
    d = lax.axis_index("dp")
    z, x = d // 2, d % 2
    pick = lambda index: lax.dynamic_index_in_dim(parts, index, 0, keepdims=False)
    order = [2 * ((z - 1 - r) % 4) for r in range(4)]
    return [pick(at + x) for at in order], [pick(at + 1 - x) for at in order]


def joined(*arrays):
    return sum(array.astype(wide) for array in arrays).astype(low)


def sum_dp(small):
    size = lax.axis_size("dp")
    step = 1
    while step < size:
        small = small + lax.ppermute(small, "dp", [(d, d ^ step) for d in range(size)])
        step *= 2
    return small


def by_slot(groups, s):
    grid = groups.reshape((2, 2) + groups.shape[1:])
    grid = jnp.swapaxes(grid, 0, 1)
    grid = jnp.where(s % 2 == 1, grid[::-1], grid)
    grid = jnp.where(s // 2 == 1, grid[:, ::-1], grid)
    return grid.reshape(groups.shape)


def by_index(slots, s):
    grid = slots.reshape((2, 2) + slots.shape[1:])
    grid = jnp.where(s % 2 == 1, grid[::-1], grid)
    grid = jnp.where(s // 2 == 1, grid[:, ::-1], grid)
    return jnp.swapaxes(grid, 0, 1).reshape(slots.shape)


def half_of(per):
    return -(-(-(-per // 4)) // 16) * 8


def pick_kernel(s_ref, gate_ref, up_ref, down_ref, *out_refs, owners, per, half):
    model = down_ref.shape[1]
    third = model // 3
    for choice in range(4):

        @pl.when(s_ref[0] == choice)
        def _():
            for part, out_ref in enumerate(out_refs):
                offset = (2 * choice + part) * half
                width = max(0, min(half, per - offset))
                for side, ref in enumerate((gate_ref, up_ref)):
                    pieces = []
                    for d in range(owners):
                        start = d * per + offset
                        pieces.append(ref[:, start : start + width])
                        if width < half:
                            pieces.append(jnp.zeros((ref.shape[0], half - width), ref.dtype))
                    out_ref[:, side * owners * half : (side + 1) * owners * half] = jnp.concatenate(pieces, axis=1)
                rows = down_ref[offset : offset + width, :]
                if width < half:
                    rows = jnp.concatenate([rows, jnp.zeros((half - width, model), rows.dtype)], axis=0)
                for j in range(3):
                    out_ref[j * half : (j + 1) * half, 2 * owners * half :] = rows[:, j * third : (j + 1) * third]


def pick_units(gate, up, down, s):
    owners = lax.axis_size("dp")
    rows, total = gate.shape
    per, model = down.shape
    half = half_of(per)
    if not by_ring():
        halves = []
        for part in range(2):
            start = (2 * s + part) * half
            sides = []
            for weight in (gate, up):
                padded = jnp.pad(weight.reshape(rows, owners, per), ((0, 0), (0, 0), (0, 8 * half - per)))
                sides.append(lax.dynamic_slice_in_dim(padded, start, half, 2).reshape(rows, owners * half))
            padded = jnp.pad(down, ((0, 8 * half - per), (0, 0)))
            block = lax.dynamic_slice_in_dim(padded, start, half, 0).reshape(half, 3, model // 3)
            sides.append(jnp.swapaxes(block, 0, 1).reshape(3 * half, model // 3))
            halves.append(jnp.concatenate(sides, axis=1))
        return halves
    return pl.pallas_call(
        functools.partial(pick_kernel, owners=owners, per=per, half=half),
        out_shape=[jax.ShapeDtypeStruct((rows, model), gate.dtype)] * 2,
        grid_spec=pltpu.PrefetchScalarGridSpec(
            num_scalar_prefetch=1,
            grid=(1,),
            in_specs=[pl.BlockSpec(w.shape, lambda i, s: (0, 0)) for w in (gate, up, down)],
            out_specs=[pl.BlockSpec((rows, model), lambda i, s: (0, 0))] * 2,
        ),
        name="pick_units",
    )(s.reshape(1), gate, up, down)


def place_kernel(first_ref, second_ref, gate_ref, up_ref, down_ref, *, owners, per, half):
    refs = (first_ref, second_ref)
    model = down_ref.shape[1]
    third = model // 3
    spans = []
    for choice in range(4):
        for part in range(2):
            offset = (2 * choice + part) * half
            spans.append((choice, part, offset, max(0, min(half, per - offset))))
    for side, ref in enumerate((gate_ref, up_ref)):
        for d in range(owners):
            pieces = []
            for choice, part, offset, width in spans:
                at = (side * owners + d) * half
                pieces.append(refs[part][choice, :, at : at + width].astype(wide))
            ref[:, d * per : (d + 1) * per] = jnp.concatenate(pieces, axis=1)
    for choice, part, offset, width in spans:
        for j in range(3):
            down_ref[offset : offset + width, j * third : (j + 1) * third] = refs[part][
                choice, j * half : j * half + width, 2 * owners * half :
            ].astype(wide)


def place_units(halves, per):
    owners = lax.axis_size("dp")
    rows, model = halves[0].shape[1:]
    half = half_of(per)
    total = per * owners
    if not by_ring():
        outs = []
        for side in range(2):
            at = side * owners * half
            grid = jnp.stack([h[:, :, at : at + owners * half].reshape(4, rows, owners, half) for h in halves], axis=3)
            flat = grid.transpose(1, 2, 0, 3, 4).reshape(rows, owners, 8 * half)[:, :, :per]
            outs.append(flat.reshape(rows, total).astype(wide))
        grid = jnp.stack([h[:, :, 2 * owners * half :].reshape(4, 3, half, model // 3) for h in halves], axis=1)
        outs.append(grid.transpose(0, 1, 3, 2, 4).reshape(8 * half, model)[:per].astype(wide))
        return outs
    return pl.pallas_call(
        functools.partial(place_kernel, owners=owners, per=per, half=half),
        out_shape=[
            jax.ShapeDtypeStruct((rows, total), wide),
            jax.ShapeDtypeStruct((rows, total), wide),
            jax.ShapeDtypeStruct((per, model), wide),
        ],
        name="place_units",
    )(*halves)


def load_blocks(place_ref, block_refs, moves, sems):
    copies = []
    for k, ref in enumerate(block_refs):
        for source, target in moves(ref, place_ref[k]):
            copies.append(pltpu.make_async_copy(source, target, sems.at[len(copies)]))
    for copy in copies:
        copy.start()
    for copy in copies:
        copy.wait()


def rows_at(index, size):
    return pl.ds(pl.multiple_of(index * size, size), size)


def project_kernel(place_ref, *refs, ring, inner, slots):
    token_refs, refs = refs[:4], refs[4:]
    count = 8 if ring else 1
    block_refs, refs = refs[:count], refs[count:]
    qkv_ref, normed_ref, weight_ref, gain_ref, taken = refs[:5]
    step = pl.program_id(0)

    @pl.when(step == 0)
    def _():
        if ring:
            rows = block_refs[0].shape[0]
            load_blocks(
                place_ref, block_refs, lambda ref, owner: [(ref, weight_ref.at[rows_at(owner, rows), :])], refs[5]
            )
        else:
            weight_ref[...] = block_refs[0][...]
        base = 3 * inner // lanes * lanes
        turned = weight_ref[:, base : base + lanes].astype(wide).T
        gain_ref[...] = turned[3 * inner - base : 3 * inner - base + 8]

    for slot in range(4):

        @pl.when(step % slots == slot)
        def _():
            taken[...] = token_refs[slot][0]

    features = taken[...].astype(wide)
    inverse = lax.rsqrt(jnp.mean(features * features, axis=-1, keepdims=True) + epsilon)
    normed = (features * inverse * gain_ref[0:1, :]).astype(low)
    normed_ref[...] = normed
    columns = 3 * inner
    qkv_ref[...] = jnp.dot(normed, weight_ref[:, :columns], preferred_element_type=wide).astype(low)


def project_heads(tokens, blocks, order, inner):
    micro_count, rows, model = tokens[0].shape
    ring = by_ring()
    columns = blocks[0].shape[1]
    total = micro_count * 4 * rows
    whole = pl.BlockSpec((model, columns), lambda i, p: (0, 0))
    return pl.pallas_call(
        functools.partial(project_kernel, ring=ring, inner=inner, slots=4),
        out_shape=[
            jax.ShapeDtypeStruct((total, 3 * inner), low),
            jax.ShapeDtypeStruct((total, model), low),
            jax.ShapeDtypeStruct((model, columns), low),
            jax.ShapeDtypeStruct((8, model), wide),
        ],
        grid_spec=pltpu.PrefetchScalarGridSpec(
            num_scalar_prefetch=1,
            grid=(micro_count * 4,),
            in_specs=[pl.BlockSpec((1, rows, model), lambda i, p: (i // 4, 0, 0))] * 4
            + ([pl.BlockSpec(memory_space=pl.ANY)] * 8 if ring else [whole]),
            out_specs=[
                pl.BlockSpec((rows, 3 * inner), lambda i, p: (i, 0)),
                pl.BlockSpec((rows, model), lambda i, p: (i, 0)),
                whole,
                pl.BlockSpec((8, model), lambda i, p: (0, 0)),
            ],
            scratch_shapes=[pltpu.VMEM((rows, model), low)] + ([pltpu.SemaphoreType.DMA((8,))] if ring else []),
        ),
        cost_estimate=pl.CostEstimate(
            flops=6 * total * model * inner, transcendentals=0, bytes_accessed=4 * total * model + 2 * model * columns
        ),
        name="project_heads",
    )(order, *tokens, *blocks)


def mix_kernel(*refs, slots):
    token_refs, part_refs = refs[:4], refs[4:8]
    mix_ref, gain_ref = refs[8:10]
    ffn_ref, middle_ref, attended_ref, taken = refs[-4:]
    step = pl.program_id(0)
    for slot in range(4):

        @pl.when(step == slot)
        def _():
            taken[...] = token_refs[slot][0]

    attended = jnp.concatenate([ref[...] for ref in part_refs], axis=1)
    middle = taken[...].astype(wide) + jnp.dot(attended, mix_ref[...], preferred_element_type=wide)
    inverse = lax.rsqrt(jnp.mean(middle * middle, axis=-1, keepdims=True) + epsilon)
    ffn_ref[...] = (middle * inverse * gain_ref[1:2, :]).astype(low)

    @pl.when(step == 0)
    def _():
        middle_ref[...] = middle
        attended_ref[...] = attended


def mix_heads(tokens, parts, mix, gains, micro, before):
    micro_count, rows, model = tokens[0].shape
    inner = parts[0].shape[1]
    own = lambda i: (0, 0)
    swaps = (0, 1, 2, 3)
    return pl.pallas_call(
        functools.partial(mix_kernel, slots=4),
        out_shape=[
            jax.ShapeDtypeStruct((micro_count * 4 * rows, model), low),
            jax.ShapeDtypeStruct((rows, model), wide),
            jax.ShapeDtypeStruct((rows, 4 * inner), low),
        ],
        grid=(4,),
        in_specs=[pl.BlockSpec((1, rows, model), lambda i: (micro, 0, 0))] * 4
        + [pl.BlockSpec((rows, inner), lambda i, k=k: (i ^ k, 0)) for k in swaps]
        + [pl.BlockSpec(mix.shape, own), pl.BlockSpec(gains.shape, own)]
        + ([] if before is None else [pl.BlockSpec(memory_space=pl.ANY)]),
        out_specs=[
            pl.BlockSpec((rows, model), lambda i: (i + 4 * micro, 0)),
            pl.BlockSpec((rows, model), own),
            pl.BlockSpec((rows, 4 * inner), own),
        ],
        scratch_shapes=[pltpu.VMEM((rows, model), low)],
        input_output_aliases={} if before is None else {10: 0},
        cost_estimate=pl.CostEstimate(
            flops=32 * rows * model * inner, transcendentals=0, bytes_accessed=24 * rows * model
        ),
        name="mix_heads",
    )(*tokens, *parts, mix, gains, *([] if before is None else [before]))


def slot_index(slot, s):
    return s ^ (2 * (slot % 2) + slot // 2)


def toeplitz_kernel(offsets_ref, out_ref, *, block, heads):
    for head in range(heads):
        row = jnp.broadcast_to(offsets_ref[head : head + 1, :], (block, offsets_ref.shape[1]))
        width = row.shape[1]
        rolled = pltpu.roll(row, width - block, 1, stride=1, stride_axis=0)
        out_ref[head] = rolled[:, : width - block]


def toeplitz(per_offset, block):
    heads, width = per_offset.shape
    return pl.pallas_call(
        functools.partial(toeplitz_kernel, block=block, heads=heads),
        out_shape=jax.ShapeDtypeStruct((heads, block, width - block), wide),
        name="toeplitz",
    )(per_offset)


def forward_kernel(s_ref, rows_ref, all_ref, bias_ref, out_ref, probs_ref, *, heads, size, block):
    s = s_ref[0]
    here = slot_index(pl.program_id(0), s)
    inner = heads * size
    outs = []
    for head in range(heads):
        query = rows_ref[:, head * size : (head + 1) * size]
        key = all_ref[:, inner + head * size : inner + (head + 1) * size]
        value = all_ref[:, 2 * inner + head * size : 2 * inner + (head + 1) * size]
        scores = lax.dot_general(query, key, (((1,), (1,)), ((), ())), preferred_element_type=wide)
        pieces = []
        for slot in range(4):
            start = pl.multiple_of((slot_index(slot, s) - here + 3) * block, block)
            pieces.append(scores[:, slot * block : (slot + 1) * block] + bias_ref[head, :, pl.ds(start, block)])
        scores = jnp.concatenate(pieces, axis=1)
        expo = jnp.exp(scores - jnp.max(scores, axis=-1, keepdims=True))
        probs = (expo * (1.0 / jnp.sum(expo, axis=-1, keepdims=True))).astype(low)
        probs_ref[head] = probs
        outs.append(jnp.dot(probs, value, preferred_element_type=wide))
    out_ref[...] = jnp.concatenate(outs, axis=1).astype(low)


def attend_forward(mixed, bias, s, heads, micro, length):
    columns = mixed.shape[1]
    inner = columns // 3
    block = length // 4
    return pl.pallas_call(
        functools.partial(forward_kernel, heads=heads, size=inner // heads, block=block),
        out_shape=[
            jax.ShapeDtypeStruct((length, inner), low),
            jax.ShapeDtypeStruct((heads, length, length), low),
        ],
        grid_spec=pltpu.PrefetchScalarGridSpec(
            num_scalar_prefetch=1,
            grid=(4,),
            in_specs=[
                pl.BlockSpec((block, columns), lambda i, s: (i + 4 * micro, 0)),
                pl.BlockSpec((length, columns), lambda i, s: (micro, 0)),
                pl.BlockSpec(bias.shape, lambda i, s: (0, 0, 0)),
            ],
            out_specs=[
                pl.BlockSpec((block, inner), lambda i, s: (i, 0)),
                pl.BlockSpec((heads, block, length), lambda i, s: (0, i, 0)),
            ],
        ),
        cost_estimate=pl.CostEstimate(
            flops=16 * length * length * inner, transcendentals=heads * length * length,
            bytes_accessed=2 * heads * length * length + bias.size * 4,
        ),
        name="attend_forward",
    )(s.reshape(1), mixed, mixed, bias)


def backward_kernel(
    s_ref, rows_ref, all_ref, grad_ref, probs_ref, out_ref, sums_ref, key_ref, value_ref, *, heads, size, block
):
    s = s_ref[0]
    step = pl.program_id(0)
    here = slot_index(step, s)
    inner = heads * size

    @pl.when(step == 0)
    def _():
        sums_ref[...] = jnp.zeros_like(sums_ref)
        key_ref[...] = jnp.zeros_like(key_ref)
        value_ref[...] = jnp.zeros_like(value_ref)

    outs = []
    for head in range(heads):
        query = rows_ref[:, head * size : (head + 1) * size]
        key = all_ref[:, inner + head * size : inner + (head + 1) * size]
        value = all_ref[:, 2 * inner + head * size : 2 * inner + (head + 1) * size]
        grad = grad_ref[:, head * size : (head + 1) * size]
        probs_low = probs_ref[head]
        probs = probs_low.astype(wide)
        prob_grad = lax.dot_general(grad, value, (((1,), (1,)), ((), ())), preferred_element_type=wide)
        centred = jnp.sum(probs * prob_grad, axis=-1, keepdims=True)
        score_low = (probs * (prob_grad - centred)).astype(low)
        outs.append(jnp.dot(score_low, key, preferred_element_type=wide))
        key_ref[head] += lax.dot_general(query, score_low, (((0,), (0,)), ((), ())), preferred_element_type=wide)
        value_ref[head] += lax.dot_general(grad, probs_low, (((0,), (0,)), ((), ())), preferred_element_type=wide)
        for slot in range(4):
            start = pl.multiple_of((slot_index(slot, s) - here + 3) * block, block)
            sums_ref[head, :, pl.ds(start, block)] += score_low[:, slot * block : (slot + 1) * block].astype(wide)
    at = pl.multiple_of(step * block, block)
    out_ref[pl.ds(at, block), :inner] = jnp.concatenate(outs, axis=1).astype(low)

    @pl.when(step == 3)
    def _():
        turned = [key_ref[head].T for head in range(heads)] + [value_ref[head].T for head in range(heads)]
        out_ref[:, inner:] = jnp.concatenate(turned, axis=1).astype(low)


def attend_backward(mixed, grad, probs, s, heads, micro):
    columns = mixed.shape[1]
    length = probs.shape[1]
    inner = columns // 3
    block = length // 4
    size = inner // heads
    return pl.pallas_call(
        functools.partial(backward_kernel, heads=heads, size=size, block=block),
        out_shape=[
            jax.ShapeDtypeStruct((length, columns), low),
            jax.ShapeDtypeStruct((heads, block, 2 * length - block), wide),
        ],
        grid_spec=pltpu.PrefetchScalarGridSpec(
            num_scalar_prefetch=1,
            grid=(4,),
            in_specs=[
                pl.BlockSpec((block, columns), lambda i, s: (i + 4 * micro, 0)),
                pl.BlockSpec((length, columns), lambda i, s: (micro, 0)),
                pl.BlockSpec((block, inner), lambda i, s: (i, 0)),
                pl.BlockSpec((heads, block, length), lambda i, s: (0, i, 0)),
            ],
            out_specs=[
                pl.BlockSpec((length, columns), lambda i, s: (0, 0)),
                pl.BlockSpec((heads, block, 2 * length - block), lambda i, s: (0, 0, 0)),
            ],
            scratch_shapes=[pltpu.VMEM((heads, size, length), wide), pltpu.VMEM((heads, size, length), wide)],
        ),
        cost_estimate=pl.CostEstimate(
            flops=32 * length * length * inner, transcendentals=0,
            bytes_accessed=2 * heads * length * length + heads * block * length * 8,
        ),
        name="attend_backward",
    )(s.reshape(1), mixed, mixed, grad, probs)


def diagonal_kernel(*refs, heads, block):
    out_ref = refs[-1]
    width = refs[0].shape[2] + block
    for head in range(heads):
        total = refs[0][head]
        for ref in refs[1:-1]:
            total = total + ref[head]
        total = jnp.concatenate([total, jnp.zeros((block, block), wide)], axis=1)
        rows = block
        while rows > 8:
            rows //= 2
            total = total[:rows] + pltpu.roll(total[rows:], width - rows, 1)
        total = pltpu.roll(total, block, 1)
        line = total[0:1]
        for row in range(1, 8):
            line = line + pltpu.roll(total[row : row + 1], width - row, 1)
        out_ref[head : head + 1, :] = line


def diagonal_sums(sums):
    heads, block, width = sums[0].shape
    return pl.pallas_call(
        functools.partial(diagonal_kernel, heads=heads, block=block),
        out_shape=jax.ShapeDtypeStruct((heads, width + block), wide),
        name="diagonal_sums",
    )(*sums)


def ffn_kernel(place_ref, *refs, ring, first, width):
    x_ref, refs = refs[0], refs[1:]
    g_count = 4 if first else 1
    g_refs, refs = refs[:g_count], refs[g_count:]
    count = 8 if ring else 2
    block_refs, refs = refs[:count], refs[count:]
    step = pl.program_id(0)
    slot = step % 4
    if first:
        hidden_ref, grads_ref, result_ref, back_ref, all_g_ref, refs = *refs[:5], refs[5:]
    else:
        result_before, back_before, refs = *refs[:2], refs[2:]
        refs = refs[-(6 + (3 if ring else 0)) :]
        hidden_ref, grads_ref, near_result, far_result, near_back, far_back, refs = *refs[:6], refs[6:]
    if ring:
        sides_ref, down_ref, sems = refs[-3:]
        rows = block_refs[0].shape[0]
        half = rows // 3

        @pl.when(step == 0)
        def _():
            def moves(ref, owner):
                pieces = [(ref.at[:, : 2 * width], sides_ref.at[rows_at(owner, rows), :])]
                for j in range(3):
                    pieces.append(
                        (ref.at[j * half : (j + 1) * half, 2 * width :], down_ref.at[j, rows_at(owner, half), :])
                    )
                return pieces

            load_blocks(place_ref, block_refs, moves, sems)
    else:
        sides_ref, down_ref = block_refs
    third = down_ref.shape[2]
    if first:
        for k in range(4):

            @pl.when(slot == k)
            def _():
                all_g_ref[...] = g_refs[k][0]

        g_ref = all_g_ref
    else:
        g_ref = g_refs[0]
    x = x_ref[...]
    tile = min(256, width)
    for start in range(0, width, tile):
        gate_pre = jnp.dot(x, sides_ref[:, start : start + tile], preferred_element_type=wide)
        up_pre = jnp.dot(x, sides_ref[:, width + start : width + start + tile], preferred_element_type=wide)
        hidden_grad = 0.0
        for j in range(3):
            hidden_grad = hidden_grad + lax.dot_general(
                g_ref[:, j * third : (j + 1) * third],
                down_ref[j, start : start + tile, :],
                (((1,), (1,)), ((), ())),
                preferred_element_type=wide,
            )
        gelu_value, gelu_slope = gelu_pair(gate_pre)
        hidden_ref[:, start : start + tile] = (gelu_value * up_pre).astype(low)
        grads_ref[:, start : start + tile] = (hidden_grad * up_pre * gelu_slope).astype(low)
        grads_ref[:, width + start : width + start + tile] = (hidden_grad * gelu_value).astype(low)
    hidden = hidden_ref[...]
    grads = grads_ref[...]
    for j in range(3):
        span = slice(j * third, (j + 1) * third)
        back = lax.dot_general(grads, sides_ref[span, :], (((1,), (1,)), ((), ())), preferred_element_type=wide)
        result = jnp.dot(hidden, down_ref[j], preferred_element_type=wide)
        if first:
            back_ref[:, span] = back.astype(low)
            result_ref[:, span] = result.astype(low)
        else:
            back = (back + back_before[:, span].astype(wide)).astype(low)
            result = (result + result_before[:, span].astype(wide)).astype(low)

            @pl.when(slot < 2)
            def _():
                near_back[:, span] = back
                near_result[:, span] = result

            @pl.when(slot >= 2)
            def _():
                far_back[:, span] = back
                far_result[:, span] = result


def ffn_weights(blocks, model, ring, width):
    if ring:
        return blocks, [pl.BlockSpec(memory_space=pl.ANY)] * 8
    whole = blocks[0]
    owners = lax.axis_size("dp")
    half = width // owners
    down = whole[:, 2 * width :].reshape(owners, 3, half, model // 3)
    down = jnp.swapaxes(down, 0, 1).reshape(3, width, model // 3)
    sides = whole[:, : 2 * width]
    return [sides, down], [
        pl.BlockSpec(sides.shape, lambda i, p: (0, 0)),
        pl.BlockSpec(down.shape, lambda i, p: (0, 0, 0)),
    ]


def ffn_scratch(ring, model, width):
    if not ring:
        return []
    return [
        pltpu.VMEM((model, 2 * width), low),
        pltpu.VMEM((3, width, model // 3), low),
        pltpu.SemaphoreType.DMA((32,)),
    ]


def ffn_cost(tokens, model, width):
    return pl.CostEstimate(
        flops=12 * tokens * model * width,
        transcendentals=tokens * width,
        bytes_accessed=8 * tokens * model + 6 * tokens * width + 6 * model * width,
    )


def ffn_first(x, g_slots, blocks, order):
    tokens, model = x.shape
    micro_count, rows = g_slots[0].shape[:2]
    width = model // 3
    ring = by_ring()
    weights, specs = ffn_weights(blocks, model, ring, width)
    row = lambda i, p: (i, 0)
    return pl.pallas_call(
        functools.partial(ffn_kernel, ring=ring, first=True, width=width),
        out_shape=[
            jax.ShapeDtypeStruct((tokens, width), low),
            jax.ShapeDtypeStruct((tokens, 2 * width), low),
            jax.ShapeDtypeStruct((tokens, model), low),
            jax.ShapeDtypeStruct((tokens, model), low),
            jax.ShapeDtypeStruct((tokens, model), low),
        ],
        grid_spec=pltpu.PrefetchScalarGridSpec(
            num_scalar_prefetch=1,
            grid=(tokens // rows,),
            in_specs=[pl.BlockSpec((rows, model), row)]
            + [pl.BlockSpec((1, rows, model), lambda i, p: (i // 4, 0, 0))] * 4
            + specs,
            out_specs=[
                pl.BlockSpec((rows, width), row),
                pl.BlockSpec((rows, 2 * width), row),
                pl.BlockSpec((rows, model), row),
                pl.BlockSpec((rows, model), row),
                pl.BlockSpec((rows, model), row),
            ],
            scratch_shapes=ffn_scratch(ring, model, width),
        ),
        cost_estimate=ffn_cost(tokens, model, width),
        name="ffn_first",
    )(order, x, *g_slots, *weights)


def ffn_second(x, g, blocks, order, result, back, micro, rows, before):
    tokens, model = x.shape
    width = model // 3
    ring = by_ring()
    weights, specs = ffn_weights(blocks, model, ring, width)
    row = lambda i, p: (i + 4 * micro, 0)
    near = pl.BlockSpec((rows, model), lambda i, p: (jnp.minimum(i, 1), 0))
    far = pl.BlockSpec((rows, model), lambda i, p: (jnp.maximum(i - 2, 0), 0))
    at = 1 + 2 + len(weights) + 2
    return pl.pallas_call(
        functools.partial(ffn_kernel, ring=ring, first=False, width=width),
        out_shape=[jax.ShapeDtypeStruct((tokens, width), low), jax.ShapeDtypeStruct((tokens, 2 * width), low)]
        + [jax.ShapeDtypeStruct((2 * rows, model), low)] * 4,
        grid_spec=pltpu.PrefetchScalarGridSpec(
            num_scalar_prefetch=1,
            grid=(4,),
            in_specs=[pl.BlockSpec((rows, model), row)] * 2
            + specs
            + [pl.BlockSpec((rows, model), row)] * 2
            + ([] if before is None else [pl.BlockSpec(memory_space=pl.ANY)] * 2),
            out_specs=[pl.BlockSpec((rows, width), row), pl.BlockSpec((rows, 2 * width), row), near, far, near, far],
            scratch_shapes=ffn_scratch(ring, model, width),
        ),
        input_output_aliases={} if before is None else {at: 0, at + 1: 1},
        cost_estimate=ffn_cost(4 * rows, model, width),
        name="ffn_second",
    )(order, x, g, *weights, result, back, *([] if before is None else before))


def back_kernel(grad_ref, weight_ref, near_ref, far_ref):
    step = pl.program_id(0)
    columns = grad_ref.shape[1]
    out = lax.dot_general(
        grad_ref[...], weight_ref[:, :columns], (((1,), (1,)), ((), ())), preferred_element_type=wide
    ).astype(low)

    @pl.when(step < 2)
    def _():
        near_ref[...] = out

    @pl.when(step >= 2)
    def _():
        far_ref[...] = out


def heads_back(grad, weights):
    total, columns = grad.shape
    model = weights.shape[0]
    rows = total // 4
    return pl.pallas_call(
        back_kernel,
        out_shape=[jax.ShapeDtypeStruct((2 * rows, model), low)] * 2,
        grid=(4,),
        in_specs=[pl.BlockSpec((rows, columns), lambda i: (i, 0)), pl.BlockSpec(weights.shape, lambda i: (0, 0))],
        out_specs=[
            pl.BlockSpec((rows, model), lambda i: (jnp.minimum(i, 1), 0)),
            pl.BlockSpec((rows, model), lambda i: (jnp.maximum(i - 2, 0), 0)),
        ],
        cost_estimate=pl.CostEstimate(
            flops=2 * total * columns * model, transcendentals=0, bytes_accessed=2 * total * model + 2 * model * columns
        ),
        name="heads_back",
    )(grad, weights)


def per_device(
    tokens,
    query_weight,
    key_weight,
    value_weight,
    mix_weight,
    gate_weight,
    up_weight,
    down_weight,
    attn_gain,
    ffn_gain,
    bias_table,
    bucket_ids,
    out_grad,
):
    owners = lax.axis_size("dp")
    s = lax.axis_index("seq")
    core = s % 2
    micro_count = tokens.shape[0]
    local, model = tokens.shape[2:]
    bucket_count, heads = bias_table.shape
    length = bucket_ids.shape[0] // 2
    per = down_weight.shape[0]
    half = half_of(per)
    width = owners * half
    inner = query_weight.shape[1] // 4
    mix_rows = mix_weight.shape[0] // 2
    shard_rows = query_weight.shape[0]
    ring = by_ring()

    own_heads = [lax.dynamic_slice_in_dim(w, s * inner, inner, 1) for w in (query_weight, key_weight, value_weight)]
    gain_columns = jnp.pad(jnp.stack([attn_gain, ffn_gain], axis=1), ((0, 0), (0, 62)))
    mix_part = lax.dynamic_slice_in_dim(mix_weight, core * mix_rows, mix_rows, 0)
    mix_columns = jnp.swapaxes(mix_part.reshape(mix_rows, 4, model // 4), 0, 1).reshape(shard_rows, model // 4)
    head_shard = jnp.concatenate(own_heads + [gain_columns, mix_columns], axis=1)

    onehot = (jnp.arange(bucket_count, dtype=jnp.int32)[:, None] == bucket_ids[None, :]).astype(wide)
    per_offset = lax.dot_general(
        bias_table, onehot, (((0,), (0,)), ((), ())), precision=lax.Precision.HIGHEST
    )
    own_tokens, own_grad = tokens[:, 0], out_grad[:, 0]
    order = owner_order() if ring else jnp.arange(8)
    rounds = Rounds()
    add, close = rounds.add, rounds.close
    gathered = lambda shard: [lax.all_gather(shard, "dp", axis=0, tiled=True)]

    token_y = add(flip_y, own_tokens, open_end=True)
    token_core = add(flip_core, own_tokens)
    units = add(lambda *w: pick_units(*w, s), gate_weight, up_weight, down_weight)
    bias = add(lambda p: toeplitz(p, local), per_offset)
    heads_z, heads_x, first_z, first_x, second_z, second_x = ([] for unused in range(6))

    def along(shard, held, crossed, turn, cross):
        if not held:
            held.append(shard)
        if ring and turn:
            held.append(add(turn_z, held[-1]))
        if ring and cross is not None:
            crossed.append(add(flip_x, held[cross]))

    def value_of(item):
        return item.value if isinstance(item, Later) else item

    def blocks_of(shard, held, crossed):
        if not ring:
            return gathered(value_of(shard))
        return [value_of(item) for pair in zip(held, crossed) for item in pair]

    heads_at = lambda turn, cross: along(head_shard, heads_z, heads_x, turn, cross)
    first_at = lambda turn, cross: along(units.value[0], first_z, first_x, turn, cross)
    second_at = lambda turn, cross: along(units.value[1], second_z, second_x, turn, cross)
    heads_at(True, 0)
    close()
    heads_at(True, 1)
    close()
    heads_at(True, 2)
    close()
    heads_at(False, 3)
    first_at(True, None)
    token_both = add(flip_core, token_y)
    grad_y = add(flip_y, own_grad, open_end=True)
    grad_core = add(flip_core, own_grad)
    close()
    token_slots = [own_tokens, token_y.value, token_core.value, token_both.value]
    projected = add(
        lambda *a: project_heads(a[:4], a[4:], order, inner),
        *token_slots,
        *blocks_of(head_shard, heads_z, heads_x),
    )
    first_at(True, 0)
    close()
    qkv, normed, head_weights, gains = projected.value
    forward = [add(lambda q, b: attend_forward(q, b, s, heads, 0, length), qkv, bias)]
    mix_half = head_weights[:, 3 * inner + 64 :]
    mix_other = add(flip_core, mix_half)
    first_at(True, 1)
    close()
    part_y, part_core, part_both = [], [], []
    for micro in range(1, micro_count):
        forward.append(add(lambda q, b, m=micro: attend_forward(q, b, s, heads, m, length), qkv, bias))
        part_y.append(add(flip_y, forward[micro - 1].value[0]))
        part_core.append(add(flip_core, forward[micro - 1].value[0]))
        if micro == 1:
            first_at(False, 2)
            second_at(True, None)
        close()
    attended = [item.value[0] for item in forward]

    def ordered_mix(mine, other):
        halves = [m.reshape(owners, 4, mix_rows, model // 4) for m in (mine, other)]
        full_mix = jnp.stack(
            [jnp.where(core == 0, halves[0], halves[1]), jnp.where(core == 0, halves[1], halves[0])], axis=1
        )
        full_mix = full_mix.transpose(0, 1, 3, 2, 4).reshape(4, inner, model)
        return by_slot(full_mix, s).reshape(4 * inner, model)

    slot_mix = add(ordered_mix, mix_half, mix_other)
    part_y.append(add(flip_y, attended[-1]))
    part_core.append(add(flip_core, attended[-1]))
    for item in part_y[:-1]:
        part_both.append(add(flip_core, item))
    grad_both = add(flip_core, grad_y)
    first_at(False, 3)
    second_at(True, None)
    close()
    slot_mix = slot_mix.value
    grad_slots = [own_grad, grad_y.value, grad_core.value, grad_both.value]
    ffn_low = None
    saved = []
    for micro in range(micro_count):
        sources = token_slots + [attended[micro], part_y[micro].value, part_core[micro].value, part_both[micro].value]
        given = [] if ffn_low is None else [ffn_low]
        mixed = add(
            lambda *a, m=micro: mix_heads(a[:4], a[4:8], a[8], a[9], m, a[10] if m else None),
            *sources, slot_mix, gains, *given,
        )
        if micro == 0:
            part_both.append(add(flip_core, part_y[-1]))
            second_at(True, 0)
        if micro == 1:
            second_at(False, 1)
        close()
        ffn_low, middle, attended_own = mixed.value
        saved.append((forward[micro].value[1], middle, attended_own))

    first_half = add(
        lambda *a: ffn_first(a[0], a[1:5], a[5:], order),
        ffn_low, *grad_slots, *blocks_of(units.value[0], first_z, first_x),
    )
    second_at(False, 2)
    second_at(False, 3)
    close()
    first_hidden, first_grads, result, back, all_g = first_half.value
    second_blocks = blocks_of(units.value[1], second_z, second_x)

    def unit_grads(x, g, hidden, grads):
        sides = mm(x, grads, (0, 0)).reshape(owners, shard_rows, 2 * width)
        down = mm(hidden, g, (0, 0)).reshape(owners, half, 3, model // 3)
        down = jnp.swapaxes(down, 1, 2).reshape(owners, shard_rows, model // 3)
        parts = jnp.concatenate([sides, down], axis=2)
        return ring_blocks(parts) if ring else parts

    class Scatter:
        def __init__(self, parts):
            self.crossed, self.turned = [], []
            self.parts = parts
            if not ring:
                self.total = lax.psum_scatter(parts, "dp", scatter_dimension=0, tiled=False)

        def cross(self):
            if ring:
                self.crossed.append(add(flip_x, self.parts[1][len(self.crossed)]))

        def block(self, step):
            arrays = [self.parts[0][step], self.crossed[step].value]
            return arrays + ([self.turned[step - 1].value] if step else [])

        def turn(self):
            if ring:
                self.turned.append(add(lambda *a: turn_z(joined(*a)), *self.block(len(self.turned))))

        def sum(self):
            return joined(*self.block(3)) if ring else self.total.astype(low)

    first_parts = add(unit_grads, ffn_low, all_g, first_hidden, first_grads)
    close()
    first_sum = Scatter(first_parts.value)
    second, sums, arrived_back, arrived_result, away_back = None, [], [], [], []
    for micro in range(micro_count):
        given = [] if second is None else second
        outs = add(
            lambda *a, m=micro: ffn_second(
                a[0], a[1], a[2 : 2 + len(second_blocks)], order, *a[2 + len(second_blocks) : 4 + len(second_blocks)],
                m, local, list(a[4 + len(second_blocks) :]) if m else None,
            ),
            ffn_low, all_g, *second_blocks, result, back, *given,
        )
        first_sum.cross()
        if micro == 1:
            first_sum.turn()
            arrived_back.append(add(flip_core, sums[0][3]))
        close()
        second = list(outs.value[:2])
        sums.append([part.reshape(2, local, model) for part in outs.value[2:]])

    def away(near, arrived):
        return flip_y(joined(near[1], arrived[1]))

    def own_sum(near, arrived, last):
        return near[0].astype(wide) + arrived[0].astype(wide) + last.astype(wide)

    second_parts = add(unit_grads, ffn_low, all_g, *second)
    away_back.append(add(away, sums[0][2], arrived_back[0]))
    arrived_back.append(add(flip_core, sums[1][3]))
    for micro in range(micro_count):
        arrived_result.append(add(flip_core, sums[micro][1]))
    first_sum.cross()
    first_sum.turn()
    close()

    gain_one, gain_two = gains[0], gains[1]

    def after_ffn(near, arrived, last, middle, own, gain, mix):
        ffn_in = own_sum(near, arrived, last)
        normed_middle, inverse_middle = rms_forward(middle)
        middle_grad = own.astype(wide) + rms_backward(ffn_in, normed_middle, inverse_middle, gain)
        mix_in = middle_grad.astype(low)
        attended_grad = mm(mix_in, mix, (1, 1))
        parts = [attended_grad[:, k * inner : (k + 1) * inner] for k in range(4)]
        return middle_grad, mix_in, parts[0], jnp.stack([parts[1], parts[3]]), parts[2]

    def after_at(micro):
        return add(
            after_ffn, sums[micro][2], arrived_back[micro], away_back[micro], saved[micro][1], own_grad[micro],
            gain_two, slot_mix,
        )

    second_sum = Scatter(second_parts.value)
    after = [after_at(0)]
    away_back.append(add(away, sums[1][2], arrived_back[1]))
    first_sum.cross()
    first_sum.turn()
    close()
    after.append(after_at(1))
    far, near_own, near_far = [], [], []
    far.append(add(flip_y, after[0].value[3]))
    near_own.append(add(flip_core, after[0].value[4]))
    first_total = add(lambda: first_sum.sum())
    second_sum.cross()
    close()
    far.append(add(flip_y, after[1].value[3]))
    near_own.append(add(flip_core, after[1].value[4]))
    near_far.append(add(flip_core, far[0].value[1]))
    second_sum.cross()
    second_sum.turn()

    def mix_grads(*arrays):
        left, right = jnp.concatenate(arrays[:micro_count]), jnp.concatenate(arrays[micro_count:])
        grad_mix = by_index(mm(left, right, (0, 0)).reshape(4, inner, model), s).reshape(owners, 2, mix_rows, model)
        kept = lax.dynamic_index_in_dim(grad_mix, core, 1, keepdims=False)
        return kept, lax.dynamic_index_in_dim(grad_mix, 1 - core, 1, keepdims=False)

    mix_pair = add(mix_grads, *[item[2] for item in saved], *[item.value[1] for item in after])
    close()
    backward, away_result = [], []

    def attend_at(micro):
        blocks = [after[micro].value[2], far[micro].value[0], near_own[micro].value, near_far[micro].value]
        return add(
            lambda q, p, *b: attend_backward(q, jnp.concatenate(b), p, s, heads, micro), qkv, saved[micro][0], *blocks
        )

    backward.append(attend_at(0))
    near_far.append(add(flip_core, far[1].value[1]))
    away_result.append(add(away, sums[0][0], arrived_result[0]))
    mix_arrived = add(flip_core, mix_pair.value[1])
    second_sum.cross()
    second_sum.turn()
    close()
    backward.append(attend_at(1))
    away_result.append(add(away, sums[1][0], arrived_result[1]))
    mix_parts = add(lambda a, b: ring_blocks(joined(a, b)) if ring else joined(a, b), mix_pair.value[0], mix_arrived)
    second_sum.cross()
    second_sum.turn()
    close()
    mix_scatter = Scatter(mix_parts.value)
    outputs = [
        (saved[micro][1] + own_sum(sums[micro][0], arrived_result[micro].value, away_result[micro].value)).astype(low)
        for micro in range(micro_count)
    ]
    qkv_grads = [item.value[0] for item in backward]
    diagonals = [item.value[1] for item in backward]
    unit_slots = []

    def own_and_y(total):
        return [total, add(flip_y, total), add(flip_core, total)]

    unit_slots.append(own_and_y(first_total.value))
    returned = [add(heads_back, grad, head_weights) for grad in qkv_grads]
    second_total = add(lambda: second_sum.sum())
    for unused in range(4):
        mix_scatter.cross()
    close()
    unit_slots.append(own_and_y(second_total.value))
    halves = [[part.reshape(2, local, model) for part in item.value] for item in returned]
    arrived_in = [add(flip_core, far_part) for near_part, far_part in halves]

    def head_grads(x, *grads):
        parts = mm(x, jnp.concatenate(grads), (0, 0)).reshape(owners, shard_rows, 3 * inner)
        return ring_blocks(parts) if ring else parts

    head_parts = add(head_grads, normed, *qkv_grads)
    unit_slots[0].append(add(flip_core, unit_slots[0][1].value))
    mix_scatter.turn()
    close()
    head_scatter = Scatter(head_parts.value)
    away_in = [add(away, halves[0][0], arrived_in[0])]
    for unused in range(4):
        head_scatter.cross()
    unit_slots[1].append(add(flip_core, unit_slots[1][1].value))
    mix_scatter.turn()
    diagonal = add(lambda *d: diagonal_sums(d), *diagonals)
    close()
    away_in.append(add(away, halves[1][0], arrived_in[1]))
    head_scatter.turn()
    mix_scatter.turn()

    def stacked(slots):
        return by_index(jnp.stack([value_of(item) for item in slots]), s)

    placed = add(lambda a, b: place_units([a, b], per), stacked(unit_slots[0]), stacked(unit_slots[1]))
    close()
    head_scatter.turn()
    mix_total = mix_scatter.sum()
    mix_y = add(flip_y, mix_total)
    close()
    mix_sum = joined(mix_total, mix_y.value)
    mix_two = add(flip_core, mix_sum)
    head_scatter.turn()
    table_local = lax.dot_general(
        onehot, diagonal.value, (((1,), (1,)), ((), ())), precision=lax.Precision.HIGHEST
    )
    grad_bias_table = sum_dp(table_local)
    input_grads = []
    for micro in range(micro_count):
        attn_in = own_sum(halves[micro][0], arrived_in[micro].value, away_in[micro].value)
        normed_own, inverse_own = rms_forward(own_tokens[micro].astype(wide))
        input_grads.append(after[micro].value[0] + rms_backward(attn_in, normed_own, inverse_own, gain_one))
    close()
    head_total = head_scatter.sum()
    head_y = flip_y(head_total)
    head_slots = [head_total, head_y, flip_core(head_total), flip_core(head_y)]
    mix_two = mix_two.value
    grad_mix = jnp.concatenate(
        [jnp.where(core == 0, mix_sum, mix_two), jnp.where(core == 0, mix_two, mix_sum)]
    ).astype(wide)
    grad_gate, grad_up, grad_down = placed.value
    head_parts = stacked(head_slots).astype(wide)
    grad_query, grad_key, grad_value = (
        jnp.concatenate([head_parts[i, :, k * inner : (k + 1) * inner] for i in range(4)], axis=1) for k in range(3)
    )

    def gain_grad(gain, pairs):
        return sum(jnp.sum(weight.astype(wide) * grad, axis=1) for weight, grad in pairs) / gain.astype(wide)

    grad_attn_gain = gain_grad(
        attn_gain, ((query_weight, grad_query), (key_weight, grad_key), (value_weight, grad_value))
    )
    grad_ffn_gain = gain_grad(ffn_gain, ((gate_weight, grad_gate), (up_weight, grad_up)))
    return (
        jnp.stack(outputs)[:, None],
        jnp.stack(input_grads)[:, None],
        grad_query,
        grad_key,
        grad_value,
        grad_mix,
        grad_gate,
        grad_up,
        grad_down,
        grad_attn_gain,
        grad_ffn_gain,
        grad_bias_table,
    )


def solution(mesh):
    in_specs = (
        P(None, "dp", "seq", None),
        P("dp", None),
        P("dp", None),
        P("dp", None),
        P("dp", None),
        P("dp", None),
        P("dp", None),
        P("dp", None),
        P("dp"),
        P("dp"),
        P(None, "seq"),
        P(),
        P(None, "dp", "seq", None),
    )
    out_specs = (
        P(None, "dp", "seq", None),
        P(None, "dp", "seq", None),
        P("dp", None),
        P("dp", None),
        P("dp", None),
        P("dp", None),
        P("dp", None),
        P("dp", None),
        P("dp", None),
        P("dp"),
        P("dp"),
        P(None, "seq"),
    )
    return jax.shard_map(
        per_device, mesh=mesh, in_specs=in_specs, out_specs=out_specs, check_vma=False
    )
```
